32 devices in a mesh: cfg: 2 (over x), space: 8 (over z, y), diag: 2 (over core).
Axes of the slice: x: 2, y: 2, z: 4, core: 2. Of those that a mesh axis runs over, the one named last changes fastest.
Arguments:
- eigvecs: bfloat16 [8, 2, 3, 128, 16, 256], P('cfg', None, None, None, ('space', 'diag')), parts along dimension 0, may hold values from -6 to 6
- gauge_links: float32 [8, 3, 2, 3, 3, 16, 256], P('cfg', None, None, None, None, ('space', 'diag')), parts along dimension 0, may hold values from -6 to 6
- momenta: int32 [4, 3], replicated, may hold values from -2 to 2
- spin_mix: float32 [16, 4, 4], replicated, may hold values from -4 to 4
- perambulators: bfloat16 [64, 4, 2, 128, 512], P(('cfg', 'space', 'diag')), parts along dimension 0, may hold values from -0.375 to 0.375
- contraction_list: int32 [32, 3], P(('space', 'diag')), may hold values from 0 to 63, as said below
Outputs:
- diagrams: bfloat16 [64, 4, 2, 128, 512], P(('cfg', 'space', 'diag')), parts along dimension 0
The draws below stay inside these ranges and needn't reach their ends.
There are 2 independent parts, one for each index of `cfg`. The reference program is written for one: setup_inputs(seed, part) draws one part's arguments, and reference() takes and returns one part's arrays. A program takes and returns all parts, laid end to end along the dimension named above; an argument that names none is the same for every part. Nothing has to cross between parts.
Inputs may be any that keep to these rules, and one draw needn't show every extreme that they name: `contraction_list`: row j is one diagram. Column 0 is an elemental item below 64, column 1 a spin structure below 16, column 2 a perambulator q with q // 2 == j // 2; each aligned group of 2 rows names each of its 2 perambulators exactly once.
All inputs are finite; a program needn't handle non-finite values.
Results may differ from the reference program's by a relative error of at most 0.0064.
Values may be sent and summed in bfloat16 or wider, within the bound.
A program may use at most 128 MiB of HBM per device.

```python
import math
import jax
import jax.numpy as jnp
from jax import lax

TW = 4
NEV = 128
NCOL = 3
NSPIN = 4
NMOM = 4
NDISP = 4
NGAMMA = 16
LX = 16
LY = 16
DIAG_DEV = 2
PERAM_DEV = 2
NZ = 16
NITEM = 64
NDIAG = 32
NPERAM = 32


def draw_contraction_list(key, part):
    key_elem = jax.random.fold_in(key, 11)
    key_spin = jax.random.fold_in(key, 12)
    key_slot = jax.random.fold_in(key, 13)
    owners = NDIAG // DIAG_DEV
    element = jax.random.randint(key_elem, (NDIAG,), 0, NITEM)
    element = element.at[0].set(NITEM - 1)
    structure = jax.random.randint(key_spin, (NDIAG,), 0, NGAMMA)
    pattern = jnp.arange(DIAG_DEV) % PERAM_DEV
    slots = jax.vmap(lambda sub_key: jax.random.permutation(sub_key, pattern))(jax.random.split(key_slot, owners))
    peram_index = (jnp.arange(owners)[:, None] * PERAM_DEV + slots).reshape(NDIAG)
    return jnp.stack([element, structure, peram_index], 1).astype(jnp.int32)


def plant(entries, own_key, smallest, largest):
    spot = [jax.random.randint(jax.random.fold_in(own_key, axis), (), 0, length) for axis, length in enumerate(entries.shape)]
    main_axis = entries.shape.index(max(entries.shape))
    beside = spot[:main_axis] + [(spot[main_axis] + 1) % entries.shape[main_axis]] + spot[main_axis + 1:]
    return entries.at[tuple(spot)].set(smallest).at[tuple(beside)].set(largest)


def shard_levels(rng, shape, cuts, least, top_value):
    loudness, own = 1.0, jax.random.fold_in(rng, 6)
    for dim, shards_of in cuts:
        steps = jnp.exp(jax.random.uniform(jax.random.fold_in(own, dim), (shards_of,), jnp.float32, least / len(cuts), top_value / len(cuts)))
        loudness = loudness * jnp.repeat(steps, shape[dim] // shards_of).reshape([-1 if axis == dim else 1 for axis in range(len(shape))])
    return loudness


def normal_values(own_key, dims, spread, most, cuts=(), dtype=jnp.bfloat16):
    drawn = jax.random.normal(own_key, dims, jnp.float32) * spread
    if len(cuts) > 0:
        drawn = shard_levels(own_key, dims, cuts, -0.22, 0.18) * drawn
    return jnp.clip(drawn, min=-most, max=most).astype(dtype)


def setup_inputs(seed: int = 0, part: int = 0) -> dict:
    arg_keys = jax.random.split(jax.random.key(seed), 7)
    part_keys = jax.random.split(jax.random.fold_in(arg_keys[6], part), 7)
    return {
        "eigvecs": normal_values(part_keys[0], (TW, 2, NCOL, NEV, NZ, LX * LY), 1.0, 6.0, ((4, 16),)),
        "gauge_links": normal_values(part_keys[1], (TW, 3, 2, NCOL, NCOL, NZ, LX * LY), 0.6, 6.0, ((5, 16),), jnp.float32),
        "momenta": plant(jax.random.randint(arg_keys[2], (NMOM, 3), -2, 3), jax.random.fold_in(arg_keys[2], 1), -2, 2).astype(jnp.int32),
        "spin_mix": normal_values(arg_keys[3], (NGAMMA, NSPIN, NSPIN), 0.5, 4.0, (), jnp.float32),
        "perambulators": normal_values(part_keys[4], (NPERAM, NSPIN, 2, NEV, NSPIN * NEV), (2 * NEV) ** -0.5, 0.375, ((0, 16),)),
        "contraction_list": draw_contraction_list(jax.random.fold_in(arg_keys[6], 71), part),
    }


highest = lax.Precision.HIGHEST

def widen(value):
    return lax.optimization_barrier(value).astype(jnp.float32)

def color_apply(matrix, vector):
    real_rows = []
    imag_rows = []
    for row in range(3):
        real_part = jnp.zeros(vector.shape[2:], jnp.float32)
        imag_part = jnp.zeros(vector.shape[2:], jnp.float32)
        for column in range(3):
            mreal = matrix[0, row, column][None]
            mimag = matrix[1, row, column][None]
            real_part = real_part + mreal * vector[0, column] - mimag * vector[1, column]
            imag_part = imag_part + mreal * vector[1, column] + mimag * vector[0, column]
        real_rows.append(real_part)
        imag_rows.append(imag_part)
    return jnp.stack([jnp.stack(real_rows), jnp.stack(imag_rows)])

def color_adjoint(matrix, vector):
    real_rows = []
    imag_rows = []
    for row in range(3):
        real_part = jnp.zeros(vector.shape[2:], jnp.float32)
        imag_part = jnp.zeros(vector.shape[2:], jnp.float32)
        for column in range(3):
            mreal = matrix[0, column, row][None]
            mimag = matrix[1, column, row][None]
            real_part = real_part + mreal * vector[0, column] + mimag * vector[1, column]
            imag_part = imag_part + mreal * vector[1, column] - mimag * vector[0, column]
        real_rows.append(real_part)
        imag_rows.append(imag_part)
    return jnp.stack([jnp.stack(real_rows), jnp.stack(imag_rows)])

def neighbour(field, direction, offset, width):
    xcoord = jnp.arange(field.shape[-1]) % width
    if direction == 0:
        if offset == 1:
            return jnp.where(xcoord == width - 1, jnp.roll(field, width - 1, -1), jnp.roll(field, -1, -1))
        return jnp.where(xcoord == 0, jnp.roll(field, 1 - width, -1), jnp.roll(field, 1, -1))
    if direction == 1:
        return jnp.roll(field, -offset * width, -1)
    return jnp.roll(field, -offset, -2)

def phase_table(momenta, zcoord, plane, total_z):
    flat = jnp.arange(plane)
    xcoord = (flat % LX).astype(jnp.float32)
    ycoord = (flat // LX).astype(jnp.float32)
    moment = momenta.astype(jnp.float32)
    zvalue = zcoord.astype(jnp.float32)
    angle = 2.0 * math.pi * (moment[:, 0, None, None] * xcoord[None, None, :] / LX + moment[:, 1, None, None] * ycoord[None, None, :] / LY + moment[:, 2, None, None] * zvalue[None, :, None] / total_z)
    return (jnp.cos(angle), jnp.sin(angle))

def phase_apply(cosine, sine, vector):
    cos_part = cosine[:, None, None]
    sin_part = sine[:, None, None]
    real_part = cos_part * vector[0] - sin_part * vector[1]
    imag_part = sin_part * vector[0] + cos_part * vector[1]
    return jnp.stack([real_part, imag_part], 1).astype(jnp.bfloat16)

def reference(eigvecs, gauge_links, momenta, spin_mix, perambulators, contraction_list):
    total_z = eigvecs.shape[4]
    plane = eigvecs.shape[5]
    scale = 1.0 / math.sqrt(3 * plane * total_z)
    cosine, sine = phase_table(momenta, jnp.arange(total_z), plane, total_z)
    item_list = []
    for slice_index in range(TW):
        vector = eigvecs[slice_index].astype(jnp.float32)
        links_now = gauge_links[slice_index]
        shifted_list = [eigvecs[slice_index]]
        for direction in range(3):
            adjoint = color_adjoint(links_now[direction], vector).astype(jnp.bfloat16)
            forward = color_apply(links_now[direction], neighbour(vector, direction, 1, LX))
            backward = neighbour(widen(adjoint), direction, -1, LX)
            shifted_list.append((0.5 * (forward - backward)).astype(jnp.bfloat16))
        phased = widen(phase_apply(cosine, sine, vector))
        per_disp = []
        for shifted in shifted_list:
            wide = widen(shifted)
            rhs = jnp.stack([wide, jnp.stack([wide[1], -wide[0]])])
            per_disp.append(jnp.einsum('mpckzs,opclzs->mokl', phased, rhs, precision=highest))
        grams = jnp.stack(per_disp, 1)
        item_list.append(grams.reshape(NMOM * NDISP, 2, NEV, NEV))
    elementals = (jnp.concatenate(item_list) * scale).astype(jnp.bfloat16)

    def diagram(entry):
        chosen = elementals[entry[0]].astype(jnp.float32)
        upper_rows = jnp.concatenate([chosen[0], -chosen[1]], 1)
        lower_rows = jnp.concatenate([chosen[1], chosen[0]], 1)
        square = jnp.concatenate([upper_rows, lower_rows], 0)
        tau = perambulators[entry[2]].astype(jnp.float32).reshape(NSPIN, 2 * NEV, NSPIN * NEV)
        blocks = jnp.einsum('ab,sbc->sac', square, tau, precision=highest)
        weights = spin_mix[entry[1]].astype(jnp.float32)
        mixed = weights[:, 0, None, None] * blocks[0][None]
        for spin in range(1, NSPIN):
            mixed = mixed + weights[:, spin, None, None] * blocks[spin][None]
        return mixed.astype(jnp.bfloat16).reshape(NSPIN, 2, NEV, NSPIN * NEV)
    return lax.map(diagram, contraction_list)
```

```python
import functools
import math

import jax
import jax.numpy as jnp
from jax import lax
from jax.experimental import pallas as pl
from jax.experimental.pallas import tpu as pltpu
from jax.sharding import PartitionSpec as P

LX = 16
LY = 16
NDISP = 4
CHUNK = 16
MESH = pl.DeviceIdType.MESH
NT = (((1,), (1,)), ((), ()))
f32 = jnp.float32
bf16 = jnp.bfloat16


def elemental_kernel(
    dims, list_ref, alpha_ref, cos_ref, sin_ref, link_ref, eig_ref, out_ref,
    above, fields, lists, table, part1, recv1, part2, recv2, part3, recv3, own,
    v_send, v_recv, l_send, l_recv, l_local, s1, r1, s2, r2, s3, r3,
):
    nspace, ndiag, inner, local, slices, nvec, plane, factor = dims
    ndev = nspace * ndiag
    outer = nspace // inner
    space = lax.axis_index("space")
    core = lax.axis_index("diag")
    cfg = lax.axis_index("cfg")
    me = space * ndiag + core
    zpos = space // inner
    ypos = lax.rem(space, inner)

    def device(index):
        return (cfg, index // ndiag, lax.rem(index, ndiag))

    barrier = pltpu.get_barrier_semaphore()

    @pl.loop(1, ndev)
    def _(k):
        pl.semaphore_signal(
            barrier, inc=1, device_id=device(lax.rem(me + k, ndev)), device_id_type=MESH
        )

    pl.semaphore_wait(barrier, ndev - 1)

    def v_copy(t):
        return pltpu.make_async_remote_copy(
            src_ref=eig_ref.at[t], dst_ref=above.at[t],
            send_sem=v_send.at[t], recv_sem=v_recv.at[t],
            device_id=device(lax.rem(me + ndev - 1, ndev)), device_id_type=MESH,
        )

    def l_copy(k):
        return pltpu.make_async_remote_copy(
            src_ref=list_ref, dst_ref=lists.at[k],
            send_sem=l_send.at[k], recv_sem=l_recv.at[k],
            device_id=device(lax.rem(me + k, ndev)), device_id_type=MESH,
        )

    @pl.loop(1, ndev)
    def _(k):
        l_copy(k).start()

    for t in range(slices):
        v_copy(t).start()
    lists[0] = list_ref[...]

    lane = lax.broadcasted_iota(jnp.int32, (CHUNK, plane), 1)
    edge = lax.rem(lane, LX) == LX - 1

    def displace(t, direction, source):
        @pl.loop(0, nvec // CHUNK)
        def _(i):
            rows = pl.multiple_of(i * CHUNK, CHUNK)
            vec = []
            for p in range(2):
                line = []
                for c in range(3):
                    v = source[t, p, c, pl.ds(rows, CHUNK), :].astype(f32)
                    if direction == 0:
                        v = jnp.where(
                            edge, pltpu.roll(v, LX - 1, 1), pltpu.roll(v, plane - 1, 1)
                        )
                    elif direction == 1:
                        v = pltpu.roll(v, plane - LX, 1)
                    line.append(v)
                vec.append(line)
            for row in range(3):
                real = imag = None
                for col in range(3):
                    mr = link_ref[t, direction, 0, row, pl.ds(col, 1), :]
                    mi = link_ref[t, direction, 1, row, pl.ds(col, 1), :]
                    re = mr * vec[0][col] - mi * vec[1][col]
                    im = mr * vec[1][col] + mi * vec[0][col]
                    real = re if real is None else real + re
                    imag = im if imag is None else imag + im
                lanes = slice(row * plane, (row + 1) * plane)
                fields[t * NDISP + direction + 1, pl.ds(rows, CHUNK), lanes] = real.astype(bf16)
                fields[
                    t * NDISP + direction + 1, pl.ds(nvec + rows, CHUNK), lanes
                ] = imag.astype(bf16)

    @pl.loop(0, slices)
    def _(t):
        for p in range(2):
            for c in range(3):
                fields[
                    t * NDISP, p * nvec:(p + 1) * nvec, c * plane:(c + 1) * plane
                ] = eig_ref[t, p, c]
        displace(t, 0, eig_ref)
        displace(t, 1, eig_ref)

    @pl.loop(1, ndev)
    def _(k):
        l_copy(k).wait()

    to_smem = pltpu.make_async_copy(lists, table, l_local)
    to_smem.start()
    to_smem.wait()

    @pl.loop(0, slices)
    def _(t):
        v_copy(t).wait()
        displace(t, 2, above)

    def item(dest, i):
        slot = lax.rem(me + ndev - dest, ndev)
        tv = table[slot, 0, 4 * i]
        tx = table[slot, 0, 4 * i + 1]
        m = table[slot, 0, 4 * i + 2]
        md = table[slot, 0, 4 * i + 3]
        ar = alpha_ref[2 * md]
        ai = alpha_ref[2 * md + 1]
        cosine = cos_ref[pl.ds(m, 1), :]
        sine = sin_ref[pl.ds(m, 1), :]
        first = second = None
        for c in range(3):
            lanes = slice(c * plane, (c + 1) * plane)
            v = fields[tv, :, lanes]
            x = fields[tx, :, lanes].astype(f32)
            xr, xi = x[:nvec], x[nvec:]
            a, b = cosine * xr, sine * xi
            g, h = cosine * xi, sine * xr
            y = jnp.concatenate([(a + b).astype(bf16), (g - h).astype(bf16)], 0)
            z = jnp.concatenate([(a - b).astype(bf16), (g + h).astype(bf16)], 0)
            d1 = lax.dot_general(v, y, NT, preferred_element_type=f32)
            d2 = lax.dot_general(z, v, NT, preferred_element_type=f32)
            first = d1 if first is None else first + d1
            second = d2 if second is None else second + d2
        g1r = first[:nvec, :nvec] + first[nvec:, nvec:]
        g1i = first[:nvec, nvec:] - first[nvec:, :nvec]
        g2r = second[:nvec, :nvec] + second[nvec:, nvec:]
        g2i = second[:nvec, nvec:] - second[nvec:, :nvec]
        return (
            (g1r - (ar * g2r - ai * g2i)) * factor,
            (g1i - (ar * g2i + ai * g2r)) * factor,
        )

    def copy1(j):
        return pltpu.make_async_remote_copy(
            src_ref=part1.at[j], dst_ref=recv1.at[j], send_sem=s1.at[j], recv_sem=r1.at[j],
            device_id=(cfg, space, 1 - core), device_id_type=MESH,
        )

    def copy2(j):
        return pltpu.make_async_remote_copy(
            src_ref=part2.at[j], dst_ref=recv2.at[j], send_sem=s2.at[j], recv_sem=r2.at[j],
            device_id=(cfg, zpos * inner + (1 - ypos), core), device_id_type=MESH,
        )

    def copy3(j):
        return pltpu.make_async_remote_copy(
            src_ref=part3.at[j], dst_ref=recv3.at[j], send_sem=s3.at[j], recv_sem=r3.at[j],
            device_id=(cfg, lax.rem(zpos + 1 + j, outer) * inner + ypos, core),
            device_id_type=MESH,
        )

    def chip_sum(j, yway):
        zway = lax.rem(zpos + 1 + lax.rem(j, outer), outer)
        chip = (zway * inner + yway) * ndiag

        @pl.loop(0, local)
        def _(i):
            real, imag = item(chip + (1 - core), i)
            part1[j, i, 0] = real.astype(bf16)
            part1[j, i, 1] = imag.astype(bf16)

        copy1(j).start()

        @pl.loop(0, local)
        def _(i):
            real, imag = item(chip + core, i)
            own[i, 0] = real
            own[i, 1] = imag

        copy1(j).wait()

    @pl.loop(0, outer)
    def _(j):
        chip_sum(j, 1 - ypos)
        part2[j] = (own[...] + recv1[j].astype(f32)).astype(bf16)
        copy2(j).start()

    @pl.loop(0, outer)
    def _(j):
        chip_sum(j + outer, ypos)
        copy2(j).wait()
        own[...] = own[...] + recv1[j + outer].astype(f32) + recv2[j].astype(f32)

        @pl.when(j < outer - 1)
        def _():
            part3[j] = own[...].astype(bf16)
            copy3(j).start()

    @pl.loop(0, outer - 1)
    def _(j):
        copy3(j).wait()
        own[...] = own[...] + recv3[j].astype(f32)

    out_ref[...] = own[...].astype(bf16)


def diagram_kernel(pick_ref, spin_ref, elem_ref, tau_ref, out_ref):
    d = pl.program_id(0)
    g = pick_ref[d, 1]
    spins = tau_ref.shape[1]
    er, ei = elem_ref[0, 0], elem_ref[0, 1]
    square = jnp.concatenate(
        [jnp.concatenate([er, -ei], 1), jnp.concatenate([ei, er], 1)], 0
    )
    width = tau_ref.shape[3]
    step = 256 if width % 256 == 0 else width
    for start in range(0, width, step):
        blocks = [
            jnp.dot(square, tau_ref[0, s, :, start:start + step], preferred_element_type=f32)
            for s in range(spins)
        ]
        for r in range(spins):
            mixed = spin_ref[g, r * spins] * blocks[0]
            for s in range(1, spins):
                mixed = mixed + spin_ref[g, r * spins + s] * blocks[s]
            out_ref[0, r, :, start:start + step] = mixed.astype(bf16)


def body(eigvecs, gauge_links, momenta, spin_mix, perambulators, contraction_list):
    slices, _, colors, nvec, depth, plane = eigvecs.shape
    assert depth == 1 and colors == 3
    nspace, ndiag = lax.axis_size("space"), lax.axis_size("diag")
    assert ndiag == 2 and nspace % 2 == 0
    inner = 2
    outer = nspace // inner
    ndev = nspace * ndiag
    position = lax.axis_index(("space", "diag"))
    total_z = ndev
    nmom = momenta.shape[0]
    scale = 1.0 / math.sqrt(3 * plane * total_z)
    flat = jnp.arange(plane)
    moment = momenta.astype(f32)
    angle = 2.0 * math.pi * (
        moment[:, 0, None] * (flat % LX).astype(f32)[None] / LX
        + moment[:, 1, None] * (flat // LX).astype(f32)[None] / LY
        + moment[:, 2, None] * position.astype(f32) / total_z
    )
    cosine, sine = jnp.cos(angle), jnp.sin(angle)
    hop = 2.0 * math.pi * moment / jnp.array([LX, LY, total_z], f32)[None]
    alpha = jnp.stack([jnp.cos(hop), -jnp.sin(hop)], -1)
    alpha = jnp.concatenate(
        [jnp.broadcast_to(jnp.array([-1.0, 0.0], f32), (nmom, 1, 2)), alpha], 1
    ).reshape(-1)
    local = contraction_list.shape[0]
    element = contraction_list[:, 0]
    per = nmom * NDISP
    t, m, d = element // per, (element // NDISP) % nmom, element % NDISP
    row = jnp.stack([t * NDISP, t * NDISP + d, m, m * NDISP + d], 1).reshape(-1)
    row = jnp.pad(row, (0, 128 - row.shape[0])).reshape(1, 128)
    vmem = pl.BlockSpec(memory_space=pltpu.VMEM)
    smem = pl.BlockSpec(memory_space=pltpu.SMEM)
    tile = (local, 2, nvec, nvec)
    dma = pltpu.SemaphoreType.DMA
    elem = pl.pallas_call(
        functools.partial(
            elemental_kernel,
            (nspace, ndiag, inner, local, slices, nvec, plane, 0.5 * scale),
        ),
        out_shape=jax.ShapeDtypeStruct(tile, bf16),
        in_specs=[vmem, smem, vmem, vmem, vmem, vmem],
        out_specs=vmem,
        scratch_shapes=[
            pltpu.VMEM((slices, 2, 3, nvec, plane), bf16),
            pltpu.VMEM((slices * NDISP, 2 * nvec, 3 * plane), bf16),
            pltpu.VMEM((ndev, 1, 128), jnp.int32),
            pltpu.SMEM((ndev, 1, 128), jnp.int32),
            pltpu.VMEM((nspace,) + tile, bf16),
            pltpu.VMEM((nspace,) + tile, bf16),
            pltpu.VMEM((outer,) + tile, bf16),
            pltpu.VMEM((outer,) + tile, bf16),
            pltpu.VMEM((outer,) + tile, bf16),
            pltpu.VMEM((outer,) + tile, bf16),
            pltpu.VMEM(tile, f32),
            dma((slices,)), dma((slices,)),
            dma((ndev,)), dma((ndev,)), dma,
            dma((nspace,)), dma((nspace,)),
            dma((outer,)), dma((outer,)),
            dma((outer,)), dma((outer,)),
        ],
        compiler_params=pltpu.CompilerParams(
            collective_id=0, has_side_effects=True, vmem_limit_bytes=48 * 1024 * 1024
        ),
    )(
        row, alpha, cosine, sine, gauge_links.reshape(slices, 3, 2, 3, 3, plane),
        eigvecs.reshape(slices, 2, 3, nvec, plane),
    )
    count, spins = perambulators.shape[:2]
    width = perambulators.shape[4]
    tau = perambulators.reshape(count, spins, 2 * nvec, width)
    pick = jnp.stack([contraction_list[:, 2] - position * count, contraction_list[:, 1]], 1)
    out = pl.pallas_call(
        diagram_kernel,
        grid_spec=pltpu.PrefetchScalarGridSpec(
            num_scalar_prefetch=2,
            grid=(local,),
            in_specs=[
                pl.BlockSpec((1, 2, nvec, nvec), lambda i, pick, spin: (i, 0, 0, 0)),
                pl.BlockSpec((1, spins, 2 * nvec, width), lambda i, pick, spin: (pick[i, 0], 0, 0, 0)),
            ],
            out_specs=pl.BlockSpec((1, spins, 2 * nvec, width), lambda i, pick, spin: (i, 0, 0, 0)),
        ),
        out_shape=jax.ShapeDtypeStruct((local, spins, 2 * nvec, width), bf16),
    )(pick, spin_mix.reshape(spin_mix.shape[0], -1), elem, tau)
    return out.reshape(local, spins, 2, nvec, width)


def solution(mesh):
    placed = (
        P("cfg", None, None, None, ("space", "diag"), None),
        P("cfg", None, None, None, None, ("space", "diag"), None),
        P(),
        P(),
        P(("cfg", "space", "diag"), None, None, None, None),
        P(("space", "diag"), None),
    )
    return jax.shard_map(
        body,
        mesh=mesh,
        in_specs=placed,
        out_specs=P(("cfg", "space", "diag"), None, None, None, None),
        check_vma=False,
    )
```

```python
import functools
import math

import jax
import jax.numpy as jnp
from jax import lax
from jax.experimental import pallas as pl
from jax.experimental.pallas import tpu as pltpu
from jax.sharding import PartitionSpec as P

LX = 16
LY = 16
NDISP = 4
CHUNK = 16
MESH = pl.DeviceIdType.MESH
NT = (((1,), (1,)), ((), ()))
f32 = jnp.float32
bf16 = jnp.bfloat16


def elemental_kernel(
    dims, list_ref, mom_ref, link_ref, eig_hbm, out_ref,
    eig_ref, cos_ref, sin_ref, ar_ref, ai_ref, above, fields, lists, table, part1, recv1, part2, recv2, part3, recv3, own,
    e_local, v_send, v_recv, l_send, l_recv, l_local, s1, r1, s2, r2, s3, r3,
):
    nspace, ndiag, inner, local, slices, nvec, plane, factor = dims
    ndev = nspace * ndiag
    outer = nspace // inner
    space = lax.axis_index("space")
    core = lax.axis_index("diag")
    cfg = lax.axis_index("cfg")
    me = space * ndiag + core
    zpos = space // inner
    ypos = lax.rem(space, inner)

    def device(index):
        return (cfg, index // ndiag, lax.rem(index, ndiag))

    def e_copy(t):
        return pltpu.make_async_copy(eig_hbm.at[t], eig_ref.at[t], e_local.at[t])

    for t in range(slices):
        e_copy(t).start()

    barrier = pltpu.get_barrier_semaphore()

    @pl.loop(1, ndev)
    def _(k):
        pl.semaphore_signal(
            barrier, inc=1, device_id=device(lax.rem(me + k, ndev)), device_id_type=MESH
        )

    column = lax.broadcasted_iota(jnp.int32, (1, 128), 1)
    packed = jnp.zeros((1, 128), jnp.int32)
    for i in range(local):
        packed = jnp.where(column == i, list_ref[i, 0], packed)
    lists[0] = packed

    nmom = mom_ref.shape[0]
    flat = lax.broadcasted_iota(jnp.int32, (1, plane), 1)
    xcoord = lax.rem(flat, LX).astype(f32)
    ycoord = lax.div(flat, LX).astype(f32)
    zcoord = lax.convert_element_type(me, f32)
    rows, hops = [], []
    for m in range(nmom):
        mom = [mom_ref[m, axis].astype(f32) for axis in range(3)]
        rows.append(
            2.0 * math.pi * (mom[0] * xcoord / LX + mom[1] * ycoord / LY + mom[2] * zcoord / ndev)
        )
        hops.append(jnp.full((1, nvec), math.pi, f32))
        for axis, size in enumerate((LX, LY, ndev)):
            hops.append(jnp.full((1, nvec), mom[axis] * (2.0 * math.pi / size), f32))
    angle = jnp.concatenate(rows, 0)
    cos_ref[...] = jnp.cos(angle)
    sin_ref[...] = jnp.sin(angle)
    hop = jnp.concatenate(hops, 0)
    plain = lax.rem(lax.broadcasted_iota(jnp.int32, hop.shape, 0), NDISP) == 0
    ar_ref[...] = jnp.where(plain, -1.0, jnp.cos(hop))
    ai_ref[...] = jnp.where(plain, 0.0, -jnp.sin(hop))

    pl.semaphore_wait(barrier, ndev - 1)

    def v_copy(t):
        return pltpu.make_async_remote_copy(
            src_ref=eig_hbm.at[t], dst_ref=above.at[t],
            send_sem=v_send.at[t], recv_sem=v_recv.at[t],
            device_id=device(lax.rem(me + ndev - 1, ndev)), device_id_type=MESH,
        )

    def l_copy(k):
        return pltpu.make_async_remote_copy(
            src_ref=lists.at[0], dst_ref=lists.at[k],
            send_sem=l_send.at[k], recv_sem=l_recv.at[k],
            device_id=device(lax.rem(me + k, ndev)), device_id_type=MESH,
        )

    for t in range(slices):
        v_copy(t).start()

    @pl.loop(1, ndev)
    def _(k):
        l_copy(k).start()

    lane = lax.broadcasted_iota(jnp.int32, (CHUNK, plane), 1)
    edge = lax.rem(lane, LX) == LX - 1

    def displace(t, direction, source):
        @pl.loop(0, nvec // CHUNK)
        def _(i):
            rows = pl.multiple_of(i * CHUNK, CHUNK)
            vec = []
            for p in range(2):
                line = []
                for c in range(3):
                    v = source[t, p, c, pl.ds(rows, CHUNK), :].astype(f32)
                    if direction == 0:
                        v = jnp.where(
                            edge, pltpu.roll(v, LX - 1, 1), pltpu.roll(v, plane - 1, 1)
                        )
                    elif direction == 1:
                        v = pltpu.roll(v, plane - LX, 1)
                    line.append(v)
                vec.append(line)
            for row in range(3):
                real = imag = None
                for col in range(3):
                    mr = link_ref[t, direction, 0, row, col]
                    mi = link_ref[t, direction, 1, row, col]
                    re = mr * vec[0][col] - mi * vec[1][col]
                    im = mr * vec[1][col] + mi * vec[0][col]
                    real = re if real is None else real + re
                    imag = im if imag is None else imag + im
                lanes = slice(row * plane, (row + 1) * plane)
                fields[t * NDISP + direction + 1, pl.ds(rows, CHUNK), lanes] = real.astype(bf16)
                fields[
                    t * NDISP + direction + 1, pl.ds(nvec + rows, CHUNK), lanes
                ] = imag.astype(bf16)

    @pl.loop(0, slices)
    def _(t):
        e_copy(t).wait()
        for p in range(2):
            for c in range(3):
                fields[
                    t * NDISP, p * nvec:(p + 1) * nvec, c * plane:(c + 1) * plane
                ] = eig_ref[t, p, c]
        displace(t, 0, eig_ref)
        displace(t, 1, eig_ref)

    @pl.loop(1, ndev)
    def _(k):
        l_copy(k).wait()

    to_smem = pltpu.make_async_copy(lists, table, l_local)
    to_smem.start()
    to_smem.wait()

    @pl.loop(0, slices)
    def _(t):
        v_copy(t).wait()
        displace(t, 2, above)

    def item(dest, i):
        slot = lax.rem(me + ndev - dest, ndev)
        entry = table[slot, 0, i]
        time = lax.div(entry, nmom * NDISP)
        m = lax.rem(lax.div(entry, NDISP), nmom)
        d = lax.rem(entry, NDISP)
        ar = ar_ref[pl.ds(m * NDISP + d, 1), :]
        ai = ai_ref[pl.ds(m * NDISP + d, 1), :]
        cosine = cos_ref[pl.ds(m, 1), :]
        sine = sin_ref[pl.ds(m, 1), :]
        cosine = jnp.concatenate([cosine] * 3, 1)
        sine = jnp.concatenate([sine] * 3, 1)
        v = fields[time * NDISP]
        x = fields[time * NDISP + d].astype(f32)
        xr, xi = x[:nvec], x[nvec:]
        a, b = cosine * xr, sine * xi
        g, h = cosine * xi, sine * xr
        y = jnp.concatenate([(a + b).astype(bf16), (g - h).astype(bf16)], 0)
        z = jnp.concatenate([(a - b).astype(bf16), (g + h).astype(bf16)], 0)
        first = lax.dot_general(v, y, NT, preferred_element_type=f32)
        second = lax.dot_general(z, v, NT, preferred_element_type=f32)
        g1r = first[:nvec, :nvec] + first[nvec:, nvec:]
        g1i = first[:nvec, nvec:] - first[nvec:, :nvec]
        g2r = second[:nvec, :nvec] + second[nvec:, nvec:]
        g2i = second[:nvec, nvec:] - second[nvec:, :nvec]
        return (
            (g1r - (ar * g2r - ai * g2i)) * factor,
            (g1i - (ar * g2i + ai * g2r)) * factor,
        )

    def copy1(j):
        return pltpu.make_async_remote_copy(
            src_ref=part1.at[j], dst_ref=recv1.at[j], send_sem=s1.at[j], recv_sem=r1.at[j],
            device_id=(cfg, space, 1 - core), device_id_type=MESH,
        )

    def copy2(j):
        return pltpu.make_async_remote_copy(
            src_ref=part2.at[j], dst_ref=recv2.at[j], send_sem=s2.at[j], recv_sem=r2.at[j],
            device_id=(cfg, zpos * inner + (1 - ypos), core), device_id_type=MESH,
        )

    def copy3(j):
        return pltpu.make_async_remote_copy(
            src_ref=part3.at[j], dst_ref=recv3.at[j], send_sem=s3.at[j], recv_sem=r3.at[j],
            device_id=(cfg, lax.rem(zpos + 1 + j, outer) * inner + ypos, core),
            device_id_type=MESH,
        )

    def target(j):
        zway = lax.rem(zpos + 1 + lax.rem(j, outer), outer)
        yway = lax.rem(1 - ypos + j // outer, inner)
        return (zway * inner + yway) * ndiag

    def send_partner(j):
        for i in range(local):
            real, imag = item(target(j) + (1 - core), i)
            part1[j, i, 0] = real.astype(bf16)
            part1[j, i, 1] = imag.astype(bf16)
        copy1(j).start()

    def chip_sum(j):
        for i in range(local):
            real, imag = item(target(j) + core, i)
            own[j, i, 0] = real
            own[j, i, 1] = imag
        copy1(j).wait()

    send_partner(0)

    @pl.loop(0, outer)
    def _(j):
        send_partner(j + 1)
        chip_sum(j)
        part2[j] = (own[j] + recv1[j].astype(f32)).astype(bf16)
        copy2(j).start()

    @pl.loop(0, outer - 1)
    def _(j):
        k = j + outer
        send_partner(k + 1)
        chip_sum(k)
        copy2(j).wait()
        part3[j] = (own[k] + recv1[k].astype(f32) + recv2[j].astype(f32)).astype(bf16)
        copy3(j).start()

    last = nspace - 1
    chip_sum(last)
    copy2(outer - 1).wait()
    own[last] = own[last] + recv1[last].astype(f32) + recv2[outer - 1].astype(f32)

    @pl.loop(0, outer - 1)
    def _(j):
        copy3(j).wait()
        own[last] = own[last] + recv3[j].astype(f32)

    out_ref[...] = own[last].astype(bf16)


def diagram_kernel(pick_ref, spin_ref, elem_ref, tau_ref, out_ref):
    d = pl.program_id(0)
    g = pick_ref[d, 1]
    spins = tau_ref.shape[1]
    er, ei = elem_ref[0, 0], elem_ref[0, 1]
    square = jnp.concatenate(
        [jnp.concatenate([er, -ei], 1), jnp.concatenate([ei, er], 1)], 0
    )
    width = tau_ref.shape[3]
    step = 256 if width % 256 == 0 else width
    for start in range(0, width, step):
        blocks = [
            jnp.dot(square, tau_ref[0, s, :, start:start + step], preferred_element_type=f32)
            for s in range(spins)
        ]
        for r in range(spins):
            mixed = spin_ref[r, 0, g] * blocks[0]
            for s in range(1, spins):
                mixed = mixed + spin_ref[r, s, g] * blocks[s]
            out_ref[0, r, :, start:start + step] = mixed.astype(bf16)


def body(eigvecs, gauge_links, momenta, spin_mix, perambulators, contraction_list):
    slices, _, colors, nvec, depth, plane = eigvecs.shape
    assert depth == 1 and colors == 3
    nspace, ndiag = lax.axis_size("space"), lax.axis_size("diag")
    assert ndiag == 2 and nspace % 2 == 0
    inner = 2
    outer = nspace // inner
    ndev = nspace * ndiag
    scale = 1.0 / math.sqrt(3 * plane * ndev)
    nmom = momenta.shape[0]
    local = contraction_list.shape[0]
    vmem = pl.BlockSpec(memory_space=pltpu.VMEM)
    smem = pl.BlockSpec(memory_space=pltpu.SMEM)
    tile = (local, 2, nvec, nvec)
    dma = pltpu.SemaphoreType.DMA
    elem = pl.pallas_call(
        functools.partial(
            elemental_kernel,
            (nspace, ndiag, inner, local, slices, nvec, plane, 0.5 * scale),
        ),
        out_shape=jax.ShapeDtypeStruct(tile, bf16),
        in_specs=[smem, smem, vmem, pl.BlockSpec(memory_space=pltpu.HBM)],
        out_specs=vmem,
        scratch_shapes=[
            pltpu.VMEM((slices, 2, 3, nvec, plane), bf16),
            pltpu.VMEM((nmom, plane), f32),
            pltpu.VMEM((nmom, plane), f32),
            pltpu.VMEM((nmom * NDISP, nvec), f32),
            pltpu.VMEM((nmom * NDISP, nvec), f32),
            pltpu.VMEM((slices, 2, 3, nvec, plane), bf16),
            pltpu.VMEM((slices * NDISP, 2 * nvec, 3 * plane), bf16),
            pltpu.VMEM((ndev, 1, 128), jnp.int32),
            pltpu.SMEM((ndev, 1, 128), jnp.int32),
            pltpu.VMEM((nspace,) + tile, bf16),
            pltpu.VMEM((nspace,) + tile, bf16),
            pltpu.VMEM((outer,) + tile, bf16),
            pltpu.VMEM((outer,) + tile, bf16),
            pltpu.VMEM((outer,) + tile, bf16),
            pltpu.VMEM((outer,) + tile, bf16),
            pltpu.VMEM((nspace,) + tile, f32),
            dma((slices,)), dma((slices,)), dma((slices,)),
            dma((ndev,)), dma((ndev,)), dma,
            dma((nspace,)), dma((nspace,)),
            dma((outer,)), dma((outer,)),
            dma((outer,)), dma((outer,)),
        ],
        compiler_params=pltpu.CompilerParams(
            collective_id=0, has_side_effects=True, vmem_limit_bytes=63 * 1024 * 1024
        ),
    )(
        contraction_list, momenta, gauge_links,
        eigvecs.reshape(slices, 2, 3, nvec, plane),
    )
    count, spins = perambulators.shape[:2]
    halves = 2
    width = perambulators.shape[4]
    tau = perambulators.reshape(count, spins, 2 * nvec, width)
    out = pl.pallas_call(
        diagram_kernel,
        grid_spec=pltpu.PrefetchScalarGridSpec(
            num_scalar_prefetch=2,
            grid=(local, halves),
            in_specs=[
                pl.BlockSpec((1, 2, nvec, nvec), lambda i, h, pick, spin: (i, 0, 0, 0)),
                pl.BlockSpec(
                    (1, spins, 2 * nvec, width // halves),
                    lambda i, h, pick, spin: (lax.rem(pick[i, 2], count), 0, 0, h),
                ),
            ],
            out_specs=pl.BlockSpec(
                (1, spins, 2 * nvec, width // halves), lambda i, h, pick, spin: (i, 0, 0, h)
            ),
        ),
        out_shape=jax.ShapeDtypeStruct((local, spins, 2 * nvec, width), bf16),
    )(contraction_list, spin_mix.transpose(1, 2, 0), elem, tau)
    return out.reshape(local, spins, 2, nvec, width)


def solution(mesh):
    placed = (
        P("cfg", None, None, None, ("space", "diag"), None),
        P("cfg", None, None, None, None, ("space", "diag"), None),
        P(),
        P(),
        P(("cfg", "space", "diag"), None, None, None, None),
        P(("space", "diag"), None),
    )
    return jax.shard_map(
        body,
        mesh=mesh,
        in_specs=placed,
        out_specs=P(("cfg", "space", "diag"), None, None, None, None),
        check_vma=False,
    )
```

```python
import functools
import math

import jax
import jax.numpy as jnp
from jax import lax
from jax.experimental import pallas as pl
from jax.experimental.pallas import tpu as pltpu
from jax.sharding import PartitionSpec as P

LX = 16
LY = 16
NDISP = 4
CHUNK = 16
MESH = pl.DeviceIdType.MESH
NT = (((1,), (1,)), ((), ()))
f32 = jnp.float32
bf16 = jnp.bfloat16


def elemental_kernel(
    dims, list_ref, mom_ref, link_ref, eig_hbm, out_ref,
    eig_ref, cos_ref, sin_ref, ar_ref, ai_ref, above, fields, lists, table, part1, recv1, part2, recv2, part3, recv3, own,
    e_local, v_send, v_recv, l_send, l_recv, l_local, s1, r1, s2, r2, s3, r3,
):
    nspace, ndiag, inner, local, slices, nvec, plane, factor = dims
    ndev = nspace * ndiag
    outer = nspace // inner
    space = lax.axis_index("space")
    core = lax.axis_index("diag")
    cfg = lax.axis_index("cfg")
    me = space * ndiag + core
    zpos = space // inner
    ypos = lax.rem(space, inner)

    def device(index):
        return (cfg, index // ndiag, lax.rem(index, ndiag))

    def e_copy(t):
        return pltpu.make_async_copy(eig_hbm.at[t], eig_ref.at[t], e_local.at[t])

    for t in range(slices):
        e_copy(t).start()

    barrier = pltpu.get_barrier_semaphore()

    @pl.loop(1, ndev)
    def _(k):
        pl.semaphore_signal(
            barrier, inc=1, device_id=device(lax.rem(me + k, ndev)), device_id_type=MESH
        )

    column = lax.broadcasted_iota(jnp.int32, (1, 128), 1)
    packed = jnp.zeros((1, 128), jnp.int32)
    for i in range(local):
        packed = jnp.where(column == i, list_ref[i, 0], packed)
    lists[0] = packed

    nmom = mom_ref.shape[0]
    flat = lax.broadcasted_iota(jnp.int32, (1, plane), 1)
    xcoord = lax.rem(flat, LX).astype(f32)
    ycoord = lax.div(flat, LX).astype(f32)
    zcoord = lax.convert_element_type(me, f32)
    rows, hops = [], []
    for m in range(nmom):
        mom = [mom_ref[m, axis].astype(f32) for axis in range(3)]
        rows.append(
            2.0 * math.pi * (mom[0] * xcoord / LX + mom[1] * ycoord / LY + mom[2] * zcoord / ndev)
        )
        hops.append(jnp.full((1, nvec), math.pi, f32))
        for axis, size in enumerate((LX, LY, ndev)):
            hops.append(jnp.full((1, nvec), mom[axis] * (2.0 * math.pi / size), f32))
    angle = jnp.concatenate(rows, 0)
    cos_ref[...] = jnp.cos(angle)
    sin_ref[...] = jnp.sin(angle)
    hop = jnp.concatenate(hops, 0)
    plain = lax.rem(lax.broadcasted_iota(jnp.int32, hop.shape, 0), NDISP) == 0
    ar_ref[...] = jnp.where(plain, -1.0, jnp.cos(hop))
    ai_ref[...] = jnp.where(plain, 0.0, -jnp.sin(hop))

    pl.semaphore_wait(barrier, ndev - 1)

    def v_copy(t):
        return pltpu.make_async_remote_copy(
            src_ref=eig_hbm.at[t], dst_ref=above.at[t],
            send_sem=v_send.at[t], recv_sem=v_recv.at[t],
            device_id=device(lax.rem(me + ndev - 1, ndev)), device_id_type=MESH,
        )

    def l_copy(k):
        return pltpu.make_async_remote_copy(
            src_ref=lists.at[0], dst_ref=lists.at[k],
            send_sem=l_send.at[k], recv_sem=l_recv.at[k],
            device_id=device(lax.rem(me + k, ndev)), device_id_type=MESH,
        )

    for t in range(slices):
        v_copy(t).start()

    @pl.loop(1, ndev)
    def _(k):
        l_copy(k).start()

    lane = lax.broadcasted_iota(jnp.int32, (CHUNK, plane), 1)
    edge = lax.rem(lane, LX) == LX - 1

    def displace(t, direction, source):
        @pl.loop(0, nvec // CHUNK)
        def _(i):
            rows = pl.multiple_of(i * CHUNK, CHUNK)
            vec = []
            for p in range(2):
                line = []
                for c in range(3):
                    v = source[t, p, c, pl.ds(rows, CHUNK), :].astype(f32)
                    if direction == 0:
                        v = jnp.where(
                            edge, pltpu.roll(v, LX - 1, 1), pltpu.roll(v, plane - 1, 1)
                        )
                    elif direction == 1:
                        v = pltpu.roll(v, plane - LX, 1)
                    line.append(v)
                vec.append(line)
            for row in range(3):
                real = imag = None
                for col in range(3):
                    mr = link_ref[t, direction, 0, row, col]
                    mi = link_ref[t, direction, 1, row, col]
                    re = mr * vec[0][col] - mi * vec[1][col]
                    im = mr * vec[1][col] + mi * vec[0][col]
                    real = re if real is None else real + re
                    imag = im if imag is None else imag + im
                lanes = slice(row * plane, (row + 1) * plane)
                fields[t * NDISP + direction + 1, pl.ds(rows, CHUNK), lanes] = real.astype(bf16)
                fields[
                    t * NDISP + direction + 1, pl.ds(nvec + rows, CHUNK), lanes
                ] = imag.astype(bf16)

    @pl.loop(0, slices)
    def _(t):
        e_copy(t).wait()
        for p in range(2):
            for c in range(3):
                fields[
                    t * NDISP, p * nvec:(p + 1) * nvec, c * plane:(c + 1) * plane
                ] = eig_ref[t, p, c]
        displace(t, 0, eig_ref)
        displace(t, 1, eig_ref)

    @pl.loop(1, ndev)
    def _(k):
        l_copy(k).wait()

    to_smem = pltpu.make_async_copy(lists, table, l_local)
    to_smem.start()
    to_smem.wait()

    @pl.loop(0, slices)
    def _(t):
        v_copy(t).wait()
        displace(t, 2, above)

    def item(dest, i):
        slot = lax.rem(me + ndev - dest, ndev)
        entry = table[slot, 0, i]
        time = lax.div(entry, nmom * NDISP)
        m = lax.rem(lax.div(entry, NDISP), nmom)
        d = lax.rem(entry, NDISP)
        ar = ar_ref[pl.ds(m * NDISP + d, 1), :]
        ai = ai_ref[pl.ds(m * NDISP + d, 1), :]
        cosine = cos_ref[pl.ds(m, 1), :]
        sine = sin_ref[pl.ds(m, 1), :]
        cosine = jnp.concatenate([cosine] * 3, 1)
        sine = jnp.concatenate([sine] * 3, 1)
        v = fields[time * NDISP]
        x = fields[time * NDISP + d].astype(f32)
        xr, xi = x[:nvec], x[nvec:]
        a, b = cosine * xr, sine * xi
        g, h = cosine * xi, sine * xr
        y = jnp.concatenate([(a + b).astype(bf16), (g - h).astype(bf16)], 0)
        z = jnp.concatenate([(a - b).astype(bf16), (g + h).astype(bf16)], 0)
        first = lax.dot_general(v, y, NT, preferred_element_type=f32)
        second = lax.dot_general(z, v, NT, preferred_element_type=f32)
        g1r = first[:nvec, :nvec] + first[nvec:, nvec:]
        g1i = first[:nvec, nvec:] - first[nvec:, :nvec]
        g2r = second[:nvec, :nvec] + second[nvec:, nvec:]
        g2i = second[:nvec, nvec:] - second[nvec:, :nvec]
        return (
            (g1r - (ar * g2r - ai * g2i)) * factor,
            (g1i - (ar * g2i + ai * g2r)) * factor,
        )

    def copy1(j):
        return pltpu.make_async_remote_copy(
            src_ref=part1.at[j], dst_ref=recv1.at[j], send_sem=s1.at[j], recv_sem=r1.at[j],
            device_id=(cfg, space, 1 - core), device_id_type=MESH,
        )

    def copy2(j):
        return pltpu.make_async_remote_copy(
            src_ref=part2.at[j], dst_ref=recv2.at[j], send_sem=s2.at[j], recv_sem=r2.at[j],
            device_id=(cfg, zpos * inner + (1 - ypos), core), device_id_type=MESH,
        )

    def copy3(j):
        return pltpu.make_async_remote_copy(
            src_ref=part3.at[j], dst_ref=recv3.at[j], send_sem=s3.at[j], recv_sem=r3.at[j],
            device_id=(cfg, lax.rem(zpos + 1 + j, outer) * inner + ypos, core),
            device_id_type=MESH,
        )

    def target(j):
        zway = lax.rem(zpos + 1 + lax.rem(j, outer), outer)
        yway = lax.rem(1 - ypos + j // outer, inner)
        return (zway * inner + yway) * ndiag

    def send_partner(j):
        for i in range(local):
            real, imag = item(target(j) + (1 - core), i)
            part1[j, i, 0] = real.astype(bf16)
            part1[j, i, 1] = imag.astype(bf16)
        copy1(j).start()

    def chip_sum(j):
        for i in range(local):
            real, imag = item(target(j) + core, i)
            own[j, i, 0] = real
            own[j, i, 1] = imag
        copy1(j).wait()

    send_partner(0)

    @pl.loop(0, outer)
    def _(j):
        send_partner(j + 1)
        chip_sum(j)
        part2[j] = (own[j] + recv1[j].astype(f32)).astype(bf16)
        copy2(j).start()

    @pl.loop(0, outer - 1)
    def _(j):
        k = j + outer
        send_partner(k + 1)
        chip_sum(k)
        copy2(j).wait()
        part3[j] = (own[k] + recv1[k].astype(f32) + recv2[j].astype(f32)).astype(bf16)
        copy3(j).start()

    last = nspace - 1
    chip_sum(last)
    copy2(outer - 1).wait()
    own[last] = own[last] + recv1[last].astype(f32) + recv2[outer - 1].astype(f32)

    @pl.loop(0, outer - 1)
    def _(j):
        copy3(j).wait()
        own[last] = own[last] + recv3[j].astype(f32)

    out_ref[...] = own[last].astype(bf16)


def diagram_kernel(pick_ref, spin_ref, elem_ref, tau_ref, out_ref):
    d = pl.program_id(0)
    g = pick_ref[d, 1]
    spins = tau_ref.shape[1]
    er, ei = elem_ref[0, 0], elem_ref[0, 1]
    square = jnp.concatenate(
        [jnp.concatenate([er, -ei], 1), jnp.concatenate([ei, er], 1)], 0
    )
    width = tau_ref.shape[3]
    step = 256 if width % 256 == 0 else width
    for start in range(0, width, step):
        blocks = [
            jnp.dot(square, tau_ref[0, s, :, start:start + step], preferred_element_type=f32)
            for s in range(spins)
        ]
        for r in range(spins):
            mixed = spin_ref[r, 0, g] * blocks[0]
            for s in range(1, spins):
                mixed = mixed + spin_ref[r, s, g] * blocks[s]
            out_ref[0, r, :, start:start + step] = mixed.astype(bf16)


def body(eigvecs, gauge_links, momenta, spin_mix, perambulators, contraction_list):
    slices, _, colors, nvec, depth, plane = eigvecs.shape
    assert depth == 1 and colors == 3
    nspace, ndiag = lax.axis_size("space"), lax.axis_size("diag")
    assert ndiag == 2 and nspace % 2 == 0
    inner = 2
    outer = nspace // inner
    ndev = nspace * ndiag
    scale = 1.0 / math.sqrt(3 * plane * ndev)
    nmom = momenta.shape[0]
    local = contraction_list.shape[0]
    vmem = pl.BlockSpec(memory_space=pltpu.VMEM)
    smem = pl.BlockSpec(memory_space=pltpu.SMEM)
    tile = (local, 2, nvec, nvec)
    dma = pltpu.SemaphoreType.DMA
    elem = pl.pallas_call(
        functools.partial(
            elemental_kernel,
            (nspace, ndiag, inner, local, slices, nvec, plane, 0.5 * scale),
        ),
        out_shape=jax.ShapeDtypeStruct(tile, bf16),
        in_specs=[smem, smem, vmem, pl.BlockSpec(memory_space=pltpu.HBM)],
        out_specs=vmem,
        scratch_shapes=[
            pltpu.VMEM((slices, 2, 3, nvec, plane), bf16),
            pltpu.VMEM((nmom, plane), f32),
            pltpu.VMEM((nmom, plane), f32),
            pltpu.VMEM((nmom * NDISP, nvec), f32),
            pltpu.VMEM((nmom * NDISP, nvec), f32),
            pltpu.VMEM((slices, 2, 3, nvec, plane), bf16),
            pltpu.VMEM((slices * NDISP, 2 * nvec, 3 * plane), bf16),
            pltpu.VMEM((ndev, 1, 128), jnp.int32),
            pltpu.SMEM((ndev, 1, 128), jnp.int32),
            pltpu.VMEM((nspace,) + tile, bf16),
            pltpu.VMEM((nspace,) + tile, bf16),
            pltpu.VMEM((outer,) + tile, bf16),
            pltpu.VMEM((outer,) + tile, bf16),
            pltpu.VMEM((outer,) + tile, bf16),
            pltpu.VMEM((outer,) + tile, bf16),
            pltpu.VMEM((nspace,) + tile, f32),
            dma((slices,)), dma((slices,)), dma((slices,)),
            dma((ndev,)), dma((ndev,)), dma,
            dma((nspace,)), dma((nspace,)),
            dma((outer,)), dma((outer,)),
            dma((outer,)), dma((outer,)),
        ],
        compiler_params=pltpu.CompilerParams(
            collective_id=0, has_side_effects=True, vmem_limit_bytes=63 * 1024 * 1024
        ),
    )(
        contraction_list, momenta, gauge_links,
        eigvecs.reshape(slices, 2, 3, nvec, plane),
    )
    count, spins = perambulators.shape[:2]
    halves = 1
    width = perambulators.shape[4]
    tau = perambulators.reshape(count, spins, 2 * nvec, width)
    out = pl.pallas_call(
        diagram_kernel,
        grid_spec=pltpu.PrefetchScalarGridSpec(
            num_scalar_prefetch=2,
            grid=(local, halves),
            in_specs=[
                pl.BlockSpec((1, 2, nvec, nvec), lambda i, h, pick, spin: (i, 0, 0, 0)),
                pl.BlockSpec(
                    (1, spins, 2 * nvec, width // halves),
                    lambda i, h, pick, spin: (lax.rem(pick[i, 2], count), 0, 0, h),
                ),
            ],
            out_specs=pl.BlockSpec(
                (1, spins, 2 * nvec, width // halves), lambda i, h, pick, spin: (i, 0, 0, h)
            ),
        ),
        out_shape=jax.ShapeDtypeStruct((local, spins, 2 * nvec, width), bf16),
    )(contraction_list, spin_mix.transpose(1, 2, 0), elem, tau)
    return out.reshape(local, spins, 2, nvec, width)


def solution(mesh):
    placed = (
        P("cfg", None, None, None, ("space", "diag"), None),
        P("cfg", None, None, None, None, ("space", "diag"), None),
        P(),
        P(),
        P(("cfg", "space", "diag"), None, None, None, None),
        P(("space", "diag"), None),
    )
    return jax.shard_map(
        body,
        mesh=mesh,
        in_specs=placed,
        out_specs=P(("cfg", "space", "diag"), None, None, None, None),
        check_vma=False,
    )
```
